32 devices in a mesh: groups: 2 (over y), snd: 4 (over z), win: 2 (over x), pt: 2 (over core).
Axes of the slice: x: 2, y: 2, z: 4, core: 2. Of those that a mesh axis runs over, the one named last changes fastest.
Arguments:
- flux_state: float32 [4, 256, 16, 128], P(('groups', 'win'), 'snd', 'pt'), parts along dimension 0, may hold values from -6 to 6
- prior_precision: float32 [4, 256, 128], P(('groups', 'win'), 'snd'), parts along dimension 0, may hold values from 0.05 to 0.5
- footprint: bfloat16 [64, 32, 128, 128], P(('groups', 'snd'), 'win'), parts along dimension 0, may hold values from -0.125 to 0.125
- tile_ids: int32 [64, 32], P(('groups', 'snd'), 'win'), parts along dimension 0, may hold values from 0 to 255, as said below
- observed: float32 [64, 128], P(('groups', 'snd')), parts along dimension 0, may hold values from -6 to 6
- obs_weight: float32 [64, 128], P(('groups', 'snd')), parts along dimension 0, may hold values from 0.1 to 1
Outputs:
- gradient: float32 [4, 256, 16, 128], P(('groups', 'win'), 'snd', 'pt'), parts along dimension 0
The draws below stay inside these ranges and needn't reach their ends.
There are 2 independent parts, one for each index of `groups`. The reference program is written for one: setup_inputs(seed, part) draws one part's arguments, and reference() takes and returns one part's arrays. A program takes and returns all parts, laid end to end along the dimension named above; each array names one. Nothing has to cross between parts.
Inputs may be any that keep to these rules, and one draw needn't show every extreme that they name: `tile_ids`: column block w (entries w * 16 to w * 16 + 15) belongs to window w. Within the 8 rows and 16 columns of one window held by one device the entries are distinct, and at most 64 of them lie among the 64 tiles t with the same t // 64; in every window one such range is named exactly 64 times by every device.
All inputs are finite; a program needn't handle non-finite values.
Results may differ from the reference program's by a relative error of at most 0.0029.
Values may be sent and summed in bfloat16 or wider, within the bound.
No kernel may reach another device: no remote copies, remote signals or barrier semaphores. Data moves between devices by JAX's collectives and lax.ppermute only.
A program may use at most 64 MiB of HBM per device.

```python
import math
import jax
import jax.numpy as jnp
from jax import lax

TILE = 128
P_SIZE = 16
K = 16
SB_DEV = 8
NT_DEV = 64
SHARDS = 4
WINDOWS = 2
NT_W = 256
SOUND_BLOCKS = 32


def draw_tile_ids(key, part):
    ref_count = SB_DEV * K
    capacity = min(NT_DEV, max(2, 3 * ref_count // SHARDS))
    others = max(SHARDS - 1, 1)

    def one_device(shard, window):
        window_key = jax.random.fold_in(key, 1000 + window)
        hot_owner = jax.random.randint(window_key, (), 0, SHARDS)
        device_key = jax.random.fold_in(window_key, 7 + shard)
        offset_key, order_key = jax.random.split(device_key)
        position = jnp.arange(ref_count, dtype=jnp.int32)
        beyond = jnp.maximum(position - capacity, 0)
        owner_index = jnp.where(position < capacity, hot_owner, (hot_owner + 1 + beyond % others) % SHARDS)
        rank_in_owner = jnp.where(position < capacity, position, beyond // others)
        offsets = jax.random.randint(offset_key, (SHARDS,), 0, NT_DEV)
        local_tile = (offsets[owner_index] + rank_in_owner) % NT_DEV
        tile_index = owner_index * NT_DEV + local_tile
        order = jax.random.permutation(order_key, ref_count)
        return tile_index[order].reshape(SB_DEV, K)
    shard_range = jnp.arange(SHARDS, dtype=jnp.int32)
    window_range = jnp.arange(WINDOWS, dtype=jnp.int32)
    table = jax.vmap(jax.vmap(one_device, in_axes=(None, 0)), in_axes=(0, None))(shard_range, window_range)
    return table.transpose(0, 2, 1, 3).reshape(SHARDS * SB_DEV, WINDOWS * K).astype(jnp.int32)


def shard_levels(own_key, shape, cuts, least, high):
    factor_of = 1.0
    for axis_at, blocks in cuts:
        steps = jax.random.uniform(jax.random.fold_in(jax.random.fold_in(own_key, 6), axis_at), (blocks,), jnp.float32, least / len(cuts), high / len(cuts))
        factor_of = factor_of * jnp.repeat(jnp.exp(steps), shape[axis_at] // blocks).reshape((-1,) + (1,) * (len(shape) - 1 - axis_at))
    return factor_of


def bell_draw(stream_key, dims, deviation, bound, pieces=(), kind=jnp.bfloat16):
    entries = deviation * jax.random.normal(stream_key, dims, jnp.float32)
    if pieces:
        entries = entries * shard_levels(stream_key, dims, pieces, -0.22, 0.18)
    return jnp.clip(entries, -bound, bound).astype(kind)


def setup_inputs(seed: int = 0, part: int = 0) -> dict:
    streams_of = jax.random.split(jax.random.key(seed), 7)
    own_keys = jax.random.split(jax.random.fold_in(streams_of[6], part), 7)
    return {
        "flux_state": bell_draw(own_keys[0], (WINDOWS, NT_W, P_SIZE, TILE), 1.0, 6.0, ((0, 2), (1, 4), (2, 2)), jnp.float32),
        "prior_precision": jnp.clip(jnp.exp(math.log(0.5) - 2.3025851 * jax.random.uniform(own_keys[1], (WINDOWS, NT_W, TILE), jnp.float32) ** shard_levels(own_keys[1], (WINDOWS, NT_W, TILE), ((0, 2), (1, 4)), -0.2, 0.2)), 0.05, 0.5),
        "footprint": bell_draw(own_keys[2], (SOUND_BLOCKS, WINDOWS * K, TILE, TILE), (K * TILE) ** -0.5, 0.125, ((0, 4), (1, 2))),
        "tile_ids": draw_tile_ids(jax.random.fold_in(jax.random.fold_in(streams_of[6], part), 71), part),
        "observed": bell_draw(own_keys[4], (SOUND_BLOCKS, TILE), 1.0, 6.0, ((0, 4),), jnp.float32),
        "obs_weight": jnp.clip(jnp.exp(math.log(1.0) - 2.3025851 * jax.random.uniform(own_keys[5], (SOUND_BLOCKS, TILE), jnp.float32) ** shard_levels(own_keys[5], (SOUND_BLOCKS, TILE), ((0, 4),), -0.2, 0.2)), 0.1, 1.0),
    }


def reference(flux_state, prior_precision, footprint, tile_ids, observed, obs_weight):
    windows, window_tiles, points, tile_cells = flux_state.shape
    tile_depth = tile_ids.shape[1] // windows
    offsets = (jnp.arange(windows * tile_depth, dtype=jnp.int32) // tile_depth) * window_tiles
    global_ids = (tile_ids + offsets[None, :]).astype(jnp.int32)
    flat_flux = flux_state.reshape(windows * window_tiles, points, tile_cells)
    rounded = flat_flux.astype(jnp.bfloat16)

    def block_term(inputs):
        footprint_row, ids_row, observed_row, weight_row = inputs
        fetched = rounded[ids_row].astype(jnp.float32)
        foot = footprint_row.astype(jnp.float32)
        modeled = jnp.einsum("ksf,kpf->ps", foot, fetched)
        residual = (weight_row[None, :] * (modeled - observed_row[None, :])).astype(jnp.bfloat16)
        return jnp.einsum("ps,ksf->kpf", residual.astype(jnp.float32), foot)

    contrib = lax.map(block_term, (footprint, global_ids, observed, obs_weight))
    summed = jnp.zeros(flat_flux.shape, jnp.float32).at[global_ids.reshape(-1)].add(
        contrib.reshape(-1, points, tile_cells))
    return summed.reshape(flux_state.shape) + prior_precision[:, :, None, :] * flux_state
```

```python
import functools

import jax
import jax.numpy as jnp
from jax import lax
from jax.experimental import pallas as pl
from jax.experimental.pallas import tpu as pltpu
from jax.sharding import PartitionSpec as P

BF16 = jnp.bfloat16
F32 = jnp.float32
VMEM = pl.BlockSpec(memory_space=pltpu.VMEM)
SMEM = pl.BlockSpec(memory_space=pltpu.SMEM)
PARAMS = pltpu.CompilerParams(vmem_limit_bytes=40 << 20)


def partner_pairs(n, step):
    if n & (n - 1) == 0:
        return [(i, i ^ step) for i in range(n)]
    return [(i, (i + step) % n) for i in range(n)]


def slot_of(n, me, owner):
    if n & (n - 1) == 0:
        return me ^ owner
    return lax.rem(me - owner + n, n)


def send_slot_of(n, me, owner):
    if n & (n - 1) == 0:
        return me ^ owner
    return lax.rem(owner - me + n, n)


def modeled_kernel(n, ids_ref, *refs):
    shards = refs[:n]
    foot_ref, out_ref, all_ref, lhs_ref = refs[n:]
    tiles = shards[0].shape[0]
    blocks, depth = ids_ref.shape
    cells = foot_ref.shape[3]
    me = lax.axis_index("snd")
    for slot in range(n):
        all_ref[pl.ds(slot * tiles, tiles)] = shards[slot][...]
    for b in range(blocks):
        for k in range(depth):
            t = ids_ref[b, k]
            owner = lax.div(t, tiles)
            at = slot_of(n, me, owner) * tiles + (t - owner * tiles)
            lhs_ref[b, :, pl.ds(k * cells, cells)] = all_ref[at]
        rhs = jnp.concatenate([foot_ref[b, k] for k in range(depth)], axis=1)
        out_ref[b] = lax.dot_general(
            lhs_ref[b], rhs, (((1,), (1,)), ((), ())), preferred_element_type=F32
        )


def gradient_kernel(n, ids_ref, mine_ref, other_ref, obs_ref, weight_ref, foot_ref, *refs):
    outs, dense_ref = refs[:n], refs[n]
    tiles = outs[0].shape[0]
    blocks, depth = ids_ref.shape
    cells = foot_ref.shape[3]
    me = lax.axis_index("snd")
    dense_ref[...] = jnp.zeros_like(dense_ref)
    for b in range(blocks):
        modeled = mine_ref[b] + other_ref[b]
        resid = (weight_ref[pl.ds(b, 1), :] * (modeled - obs_ref[pl.ds(b, 1), :])).astype(BF16)
        rhs = jnp.concatenate([foot_ref[b, k] for k in range(depth)], axis=1)
        terms = jnp.dot(resid, rhs, preferred_element_type=F32)
        for k in range(depth):
            t = ids_ref[b, k]
            owner = lax.div(t, tiles)
            at = send_slot_of(n, me, owner) * tiles + (t - owner * tiles)
            dense_ref[at] = terms[:, k * cells : (k + 1) * cells]
    for slot in range(n):
        outs[slot][...] = dense_ref[pl.ds(slot * tiles, tiles)].astype(outs[slot].dtype)


def final_kernel(n, flux_ref, prior_ref, own_ref, *refs):
    arrived, out_ref = refs[: n - 1], refs[n - 1]
    total = own_ref[...] + prior_ref[...][:, None, :] * flux_ref[...]
    for a in arrived:
        total += a[...].astype(F32)
    out_ref[...] = total


def body(flux_state, prior_precision, footprint, tile_ids, observed, obs_weight):
    n = lax.axis_size("snd")
    windows = lax.axis_size("win")
    flux = flux_state[0]
    tiles, points, cells = flux.shape
    blocks, depth, soundings, _ = footprint.shape
    rounded = flux.astype(BF16)
    shards = [rounded] + [lax.ppermute(rounded, "snd", partner_pairs(n, s)) for s in range(1, n)]

    mine = pl.pallas_call(
        functools.partial(modeled_kernel, n),
        out_shape=jax.ShapeDtypeStruct((blocks, points, soundings), F32),
        in_specs=[SMEM] + [VMEM] * (n + 1),
        out_specs=VMEM,
        scratch_shapes=[
            pltpu.VMEM((n * tiles, points, cells), BF16),
            pltpu.VMEM((blocks, points, depth * cells), BF16),
        ],
        compiler_params=PARAMS,
        name="modeled",
    )(tile_ids, *shards, footprint)

    if windows == 2:
        other = lax.ppermute(mine, "win", [(0, 1), (1, 0)])
    else:
        other = lax.psum(mine, "win") - mine
    grads = pl.pallas_call(
        functools.partial(gradient_kernel, n),
        out_shape=[jax.ShapeDtypeStruct((tiles, points, cells), F32)]
        + [jax.ShapeDtypeStruct((tiles, points, cells), BF16)] * (n - 1),
        in_specs=[SMEM] + [VMEM] * 5,
        out_specs=[VMEM] * n,
        scratch_shapes=[pltpu.VMEM((n * tiles, points, cells), F32)],
        compiler_params=PARAMS,
        name="terms",
    )(tile_ids, mine, other, observed, obs_weight, footprint)
    arrived = [lax.ppermute(grads[s], "snd", partner_pairs(n, s)) for s in range(1, n)]
    gradient = pl.pallas_call(
        functools.partial(final_kernel, n),
        out_shape=jax.ShapeDtypeStruct((tiles, points, cells), F32),
        in_specs=[VMEM] * (n + 2),
        out_specs=VMEM,
        compiler_params=PARAMS,
        name="total",
    )(flux, prior_precision[0], grads[0], *arrived)
    return gradient[None]


def solution(mesh):
    placed = (
        P(("groups", "win"), "snd", "pt", None),
        P(("groups", "win"), "snd", None),
        P(("groups", "snd"), "win", None, None),
        P(("groups", "snd"), "win"),
        P(("groups", "snd"), None),
        P(("groups", "snd"), None),
    )
    return jax.shard_map(
        body,
        mesh=mesh,
        in_specs=placed,
        out_specs=P(("groups", "win"), "snd", "pt", None),
        check_vma=False,
    )
```

```python
import functools

import jax
import jax.numpy as jnp
from jax import lax
from jax.experimental import pallas as pl
from jax.experimental.pallas import tpu as pltpu
from jax.sharding import PartitionSpec as P

BF16 = jnp.bfloat16
F32 = jnp.float32
VMEM = pl.BlockSpec(memory_space=pltpu.VMEM)
ANY = pl.BlockSpec(memory_space=pl.ANY)
SMEM = pl.BlockSpec(memory_space=pltpu.SMEM)
PARAMS = pltpu.CompilerParams(vmem_limit_bytes=40 << 20)


def shifted_pairs(n, step):
    return [(i, (i + step) % n) for i in range(n)]


def stage_kernel(ids_ref, foot_ref, ids_out, foot_out, sems):
    copies = [
        pltpu.make_async_copy(foot_ref, foot_out, sems.at[0]),
        pltpu.make_async_copy(ids_ref, ids_out, sems.at[1]),
    ]
    for copy in copies:
        copy.start()
    for copy in copies:
        copy.wait()


def modeled_kernel(n, ids_ref, *refs):
    shards = refs[:n]
    foot_ref, out_ref, all_ref, lhs_ref = refs[n:]
    tiles = shards[0].shape[0]
    blocks, depth = ids_ref.shape
    cells = foot_ref.shape[3]
    me = lax.axis_index("snd")
    for slot in range(n):
        all_ref[pl.ds(slot * tiles, tiles)] = shards[slot][...]
    for b in range(blocks):
        for k in range(depth):
            t = ids_ref[b, k]
            owner = lax.div(t, tiles)
            at = lax.rem(me - owner + n, n) * tiles + (t - owner * tiles)
            lhs_ref[b, :, pl.ds(k * cells, cells)] = all_ref[at]
        rhs = jnp.concatenate([foot_ref[b, k] for k in range(depth)], axis=1)
        out_ref[b] = lax.dot_general(
            lhs_ref[b], rhs, (((1,), (1,)), ((), ())), preferred_element_type=F32
        )


def gradient_kernel(n, ids_ref, mine_ref, other_ref, obs_ref, weight_ref, foot_ref, *refs):
    outs, dense_ref = refs[:n], refs[n]
    tiles = outs[0].shape[0]
    blocks, depth = ids_ref.shape
    cells = foot_ref.shape[3]
    me = lax.axis_index("snd")
    dense_ref[...] = jnp.zeros_like(dense_ref)
    for b in range(blocks):
        modeled = mine_ref[b] + other_ref[b]
        resid = (weight_ref[pl.ds(b, 1), :] * (modeled - obs_ref[pl.ds(b, 1), :])).astype(BF16)
        rhs = jnp.concatenate([foot_ref[b, k] for k in range(depth)], axis=1)
        terms = jnp.dot(resid, rhs, preferred_element_type=F32)
        for k in range(depth):
            t = ids_ref[b, k]
            owner = lax.div(t, tiles)
            at = lax.rem(owner - me + n, n) * tiles + (t - owner * tiles)
            dense_ref[at] = terms[:, k * cells : (k + 1) * cells]
    for slot in range(n):
        outs[slot][...] = dense_ref[pl.ds(slot * tiles, tiles)].astype(outs[slot].dtype)


def final_kernel(n, flux_ref, prior_ref, own_ref, *refs):
    arrived, out_ref = refs[: n - 1], refs[n - 1]
    total = own_ref[...] + prior_ref[...][:, None, :] * flux_ref[...]
    for a in arrived:
        total += a[...].astype(F32)
    out_ref[...] = total


def body(flux_state, prior_precision, footprint, tile_ids, observed, obs_weight):
    n = lax.axis_size("snd")
    windows = lax.axis_size("win")
    flux = flux_state[0]
    tiles, points, cells = flux.shape
    blocks, depth, soundings, _ = footprint.shape
    rounded = flux.astype(BF16)
    shards = [rounded] + [lax.ppermute(rounded, "snd", shifted_pairs(n, s)) for s in range(1, n)]

    tile_ids, footprint = pl.pallas_call(
        stage_kernel,
        out_shape=[
            jax.ShapeDtypeStruct(tile_ids.shape, tile_ids.dtype),
            jax.ShapeDtypeStruct(footprint.shape, footprint.dtype),
        ],
        in_specs=[ANY] * 2,
        out_specs=[VMEM] * 2,
        scratch_shapes=[pltpu.SemaphoreType.DMA((2,))],
        compiler_params=PARAMS,
        cost_estimate=pl.CostEstimate(
            flops=0, transcendentals=0, bytes_accessed=footprint.size * 4
        ),
        name="stage",
    )(tile_ids, footprint)
    mine = pl.pallas_call(
        functools.partial(modeled_kernel, n),
        out_shape=jax.ShapeDtypeStruct((blocks, points, soundings), F32),
        in_specs=[SMEM] + [VMEM] * (n + 1),
        out_specs=VMEM,
        scratch_shapes=[
            pltpu.VMEM((n * tiles, points, cells), BF16),
            pltpu.VMEM((blocks, points, depth * cells), BF16),
        ],
        compiler_params=PARAMS,
        name="modeled",
    )(tile_ids, *shards, footprint)

    if windows == 2:
        other = lax.ppermute(mine, "win", [(0, 1), (1, 0)])
    else:
        other = lax.psum(mine, "win") - mine
    grads = pl.pallas_call(
        functools.partial(gradient_kernel, n),
        out_shape=[jax.ShapeDtypeStruct((tiles, points, cells), F32)]
        + [jax.ShapeDtypeStruct((tiles, points, cells), BF16)] * (n - 1),
        in_specs=[SMEM] + [VMEM] * 5,
        out_specs=[VMEM] * n,
        scratch_shapes=[pltpu.VMEM((n * tiles, points, cells), F32)],
        compiler_params=PARAMS,
        name="terms",
    )(tile_ids, mine, other, observed, obs_weight, footprint)
    arrived = [lax.ppermute(grads[s], "snd", shifted_pairs(n, s)) for s in range(1, n)]
    gradient = pl.pallas_call(
        functools.partial(final_kernel, n),
        out_shape=jax.ShapeDtypeStruct((tiles, points, cells), F32),
        in_specs=[VMEM] * (n + 2),
        out_specs=VMEM,
        compiler_params=PARAMS,
        name="total",
    )(flux, prior_precision[0], grads[0], *arrived)
    return gradient[None]


def solution(mesh):
    placed = (
        P(("groups", "win"), "snd", "pt", None),
        P(("groups", "win"), "snd", None),
        P(("groups", "snd"), "win", None, None),
        P(("groups", "snd"), "win"),
        P(("groups", "snd"), None),
        P(("groups", "snd"), None),
    )
    return jax.shard_map(
        body,
        mesh=mesh,
        in_specs=placed,
        out_specs=P(("groups", "win"), "snd", "pt", None),
        check_vma=False,
    )
```

```python
import functools

import jax
import jax.numpy as jnp
from jax import lax
from jax.experimental import pallas as pl
from jax.experimental.pallas import tpu as pltpu
from jax.sharding import PartitionSpec as P

BF16 = jnp.bfloat16
F32 = jnp.float32
I32 = jnp.int32
HBM = pl.BlockSpec(memory_space=pltpu.HBM)
VMEM = pl.BlockSpec(memory_space=pltpu.VMEM)
PARAMS = pltpu.CompilerParams(vmem_limit_bytes=40 << 20)
PIECES = 4


def shifted_pairs(n, step):
    return [(i, (i + step) % n) for i in range(n)]


def struct(shape, dtype):
    return jax.ShapeDtypeStruct(shape, dtype)


def in_hbm(x):
    return pltpu.with_memory_space_constraint(x, pltpu.HBM)


def round_kernel(flux_ref, out_ref, buf_ref, sems):
    size = flux_ref.shape[0] // PIECES
    pieces = [pl.ds(i * size, size) for i in range(PIECES)]
    copies = [
        pltpu.make_async_copy(flux_ref.at[at], buf_ref.at[at], sems.at[i]) for i, at in enumerate(pieces)
    ]
    for copy in copies:
        copy.start()
    for copy, at in zip(copies, pieces):
        copy.wait()
        out_ref[at] = buf_ref[at].astype(BF16)


def stage_kernel(n, tiles, ids_ref, foot_ref, take_ref, put_ref, foot_out, turned_ref, sems):
    blocks, depth = ids_ref.shape
    copies = [pltpu.make_async_copy(foot_ref.at[b], foot_out.at[b], sems.at[b]) for b in range(blocks)]
    for copy in copies:
        copy.start()
    me = lax.axis_index("snd")
    ids = ids_ref[...]
    shift = tiles.bit_length() - 1
    owner = lax.shift_right_logical(ids, shift)
    local = ids - lax.shift_left(owner, shift)
    slot = me - owner
    take_ref[...] = jnp.where(slot < 0, slot + n, slot) * tiles + local
    slot = owner - me
    put_ref[...] = jnp.where(slot < 0, slot + n, slot) * tiles + local
    for b in range(blocks):
        copies[b].wait()
        turned_ref[b] = jnp.swapaxes(foot_out[b], 1, 2)


def modeled_kernel(n, take_ref, turned_ref, *refs):
    shards = refs[:n]
    out_ref, all_ref = refs[n:]
    tiles = shards[0].shape[0]
    blocks, depth = take_ref.shape
    for slot in range(n):
        all_ref[pl.ds(slot * tiles, tiles)] = shards[slot][...]
    take = take_ref[...]
    for b in range(blocks):
        lhs = jnp.concatenate([all_ref[take[b, k]] for k in range(depth)], axis=1)
        rhs = jnp.concatenate([turned_ref[b, k] for k in range(depth)], axis=0)
        out_ref[b] = jnp.dot(lhs, rhs, preferred_element_type=F32)


def terms_kernel(n, put_ref, mine_ref, other_ref, obs_ref, weight_ref, foot_ref, *refs):
    outs, dense_ref = refs[:n], refs[n]
    tiles = outs[0].shape[0]
    blocks, depth, _, cells = foot_ref.shape
    dense_ref[...] = jnp.zeros_like(dense_ref)
    put = put_ref[...]
    for b in range(blocks):
        modeled = mine_ref[b] + other_ref[b]
        resid = (weight_ref[pl.ds(b, 1), :] * (modeled - obs_ref[pl.ds(b, 1), :])).astype(BF16)
        rhs = jnp.concatenate([foot_ref[b, k] for k in range(depth)], axis=1)
        terms = jnp.dot(resid, rhs, preferred_element_type=F32)
        for k in range(depth):
            dense_ref[put[b, k]] = terms[:, k * cells : (k + 1) * cells]
    for slot in range(n):
        outs[slot][...] = dense_ref[pl.ds(slot * tiles, tiles)].astype(outs[slot].dtype)


def total_kernel(n, flux_ref, prior_ref, own_ref, *refs):
    arrived, out_ref = refs[: n - 1], refs[n - 1]
    total = own_ref[...] + prior_ref[...][:, None, :] * flux_ref[...]
    for a in arrived:
        total += a[...].astype(F32)
    out_ref[...] = total


def body(flux_state, prior_precision, footprint, tile_ids, observed, obs_weight):
    n = lax.axis_size("snd")
    windows = lax.axis_size("win")
    flux = flux_state[0]
    tiles, points, cells = flux.shape
    blocks, depth, soundings, _ = footprint.shape
    assert tiles & (tiles - 1) == 0 and tiles % PIECES == 0
    held = (tiles, points, cells)

    rounded = pl.pallas_call(
        round_kernel,
        out_shape=struct(held, BF16),
        in_specs=[HBM],
        out_specs=VMEM,
        scratch_shapes=[pltpu.VMEM(held, F32), pltpu.SemaphoreType.DMA((PIECES,))],
        compiler_params=PARAMS,
        name="round",
    )(in_hbm(flux))
    shards = [rounded] + [lax.ppermute(rounded, "snd", shifted_pairs(n, s)) for s in range(1, n)]
    take, put, foot, turned = pl.pallas_call(
        functools.partial(stage_kernel, n, tiles),
        out_shape=[struct(tile_ids.shape, I32)] * 2 + [struct(footprint.shape, BF16)] * 2,
        in_specs=[VMEM, HBM],
        out_specs=[VMEM] * 4,
        scratch_shapes=[pltpu.SemaphoreType.DMA((blocks,))],
        compiler_params=PARAMS,
        cost_estimate=pl.CostEstimate(flops=0, transcendentals=0, bytes_accessed=footprint.size * 4),
        name="stage",
    )(tile_ids, in_hbm(footprint))
    mine = pl.pallas_call(
        functools.partial(modeled_kernel, n),
        out_shape=struct((blocks, points, soundings), F32),
        in_specs=[VMEM] * (n + 2),
        out_specs=VMEM,
        scratch_shapes=[pltpu.VMEM((n * tiles, points, cells), BF16)],
        compiler_params=PARAMS,
        name="modeled",
    )(take, turned, *shards)
    if windows == 2:
        other = lax.ppermute(mine, "win", [(0, 1), (1, 0)])
    else:
        other = lax.psum(mine, "win") - mine
    terms = pl.pallas_call(
        functools.partial(terms_kernel, n),
        out_shape=[struct(held, F32)] + [struct(held, BF16)] * (n - 1),
        in_specs=[VMEM] * 6,
        out_specs=[VMEM] * n,
        scratch_shapes=[pltpu.VMEM((n * tiles, points, cells), F32)],
        compiler_params=PARAMS,
        name="terms",
    )(put, mine, other, observed, obs_weight, foot)
    arrived = [lax.ppermute(terms[s], "snd", shifted_pairs(n, s)) for s in range(1, n)]
    gradient = pl.pallas_call(
        functools.partial(total_kernel, n),
        out_shape=struct(held, F32),
        in_specs=[VMEM] * (n + 2),
        out_specs=VMEM,
        compiler_params=PARAMS,
        name="total",
    )(flux, prior_precision[0], terms[0], *arrived)
    return gradient[None]


def solution(mesh):
    placed = (
        P(("groups", "win"), "snd", "pt", None),
        P(("groups", "win"), "snd", None),
        P(("groups", "snd"), "win", None, None),
        P(("groups", "snd"), "win"),
        P(("groups", "snd"), None),
        P(("groups", "snd"), None),
    )
    return jax.shard_map(
        body,
        mesh=mesh,
        in_specs=placed,
        out_specs=P(("groups", "win"), "snd", "pt", None),
        check_vma=False,
    )
```

```python
import functools

import jax
import jax.numpy as jnp
from jax import lax
from jax.experimental import pallas as pl
from jax.experimental.pallas import tpu as pltpu
from jax.sharding import PartitionSpec as P

BF16 = jnp.bfloat16
F32 = jnp.float32
I32 = jnp.int32
HBM = pl.BlockSpec(memory_space=pltpu.HBM)
VMEM = pl.BlockSpec(memory_space=pltpu.VMEM)
PARAMS = pltpu.CompilerParams(vmem_limit_bytes=40 << 20)
PIECES = 4


NEXT, ACROSS, LAST = (1, 2, 3, 0), (2, 3, 0, 1), (3, 0, 1, 2)
CYCLE, MIRROR, BACK = (2, 0, 3, 1), (3, 2, 1, 0), (1, 3, 0, 2)


def plans(n, cores):
    if n == 4 and cores == 2:
        shifts = (NEXT, ACROSS, LAST)
        return (shifts, (CYCLE, MIRROR, BACK)), (shifts, (MIRROR, BACK, CYCLE))
    shifts = tuple(tuple((i + s) % n for i in range(n)) for s in range(1, n))
    return (shifts,) * cores, (shifts,) * cores


def sent(x, plan, step):
    cores = len(plan)
    pairs = [(i * cores + c, to * cores + c) for c, steps in enumerate(plan) for i, to in enumerate(steps[step])]
    return lax.ppermute(x, ("snd", "pt"), pairs)


def slots(plan, owner, arriving):
    n = len(plan[0]) + 1
    me, core = lax.axis_index("snd"), lax.axis_index("pt")
    if all(to == tuple((i + s + 1) % n for i in range(n)) for steps in plan for s, to in enumerate(steps)):
        slot = me - owner if arriving else owner - me
        return jnp.where(slot < 0, slot + n, slot)
    slot = jnp.zeros_like(owner)
    for other in range(n):
        step = jnp.int32(0)
        for c, steps in enumerate(plan):
            for s, to in enumerate(steps):
                source = to.index(other)
                here = to[other] if arriving else source
                step = jnp.where((core == c) & (me == here), s + 1, step)
        slot = jnp.where(owner == other, step, slot)
    return slot


def struct(shape, dtype):
    return jax.ShapeDtypeStruct(shape, dtype)


def in_hbm(x):
    return pltpu.with_memory_space_constraint(x, pltpu.HBM)


def round_kernel(flux_ref, out_ref, buf_ref, sems):
    size = flux_ref.shape[0] // PIECES
    pieces = [pl.ds(i * size, size) for i in range(PIECES)]
    copies = [
        pltpu.make_async_copy(flux_ref.at[at], buf_ref.at[at], sems.at[i]) for i, at in enumerate(pieces)
    ]
    for copy in copies:
        copy.start()
    for copy, at in zip(copies, pieces):
        copy.wait()
        out_ref[at] = buf_ref[at].astype(BF16)


def stage_kernel(gather, spread, tiles, ids_ref, foot_ref, take_ref, put_ref, foot_out, turned_ref, sems):
    blocks, depth = ids_ref.shape
    copies = [pltpu.make_async_copy(foot_ref.at[b], foot_out.at[b], sems.at[b]) for b in range(blocks)]
    for copy in copies:
        copy.start()
    ids = ids_ref[...]
    shift = tiles.bit_length() - 1
    owner = lax.shift_right_logical(ids, shift)
    local = ids - lax.shift_left(owner, shift)
    take_ref[...] = slots(gather, owner, True) * tiles + local
    put_ref[...] = slots(spread, owner, False) * tiles + local
    for b in range(blocks):
        copies[b].wait()
        turned_ref[b] = jnp.swapaxes(foot_out[b], 1, 2)


def modeled_kernel(n, take_ref, turned_ref, *refs):
    shards = refs[:n]
    out_ref, all_ref = refs[n:]
    tiles = shards[0].shape[0]
    blocks, depth = take_ref.shape
    for slot in range(n):
        all_ref[pl.ds(slot * tiles, tiles)] = shards[slot][...]
    take = take_ref[...]
    for b in range(blocks):
        lhs = jnp.concatenate([all_ref[take[b, k]] for k in range(depth)], axis=1)
        rhs = jnp.concatenate([turned_ref[b, k] for k in range(depth)], axis=0)
        out_ref[b] = jnp.dot(lhs, rhs, preferred_element_type=F32)


def terms_kernel(n, put_ref, mine_ref, other_ref, obs_ref, weight_ref, foot_ref, *refs):
    outs, dense_ref = refs[:n], refs[n]
    tiles = outs[0].shape[0]
    blocks, depth, _, cells = foot_ref.shape
    dense_ref[...] = jnp.zeros_like(dense_ref)
    put = put_ref[...]
    for b in range(blocks):
        modeled = mine_ref[b] + other_ref[b]
        resid = (weight_ref[pl.ds(b, 1), :] * (modeled - obs_ref[pl.ds(b, 1), :])).astype(BF16)
        rhs = jnp.concatenate([foot_ref[b, k] for k in range(depth)], axis=1)
        terms = jnp.dot(resid, rhs, preferred_element_type=F32)
        for k in range(depth):
            dense_ref[put[b, k]] = terms[:, k * cells : (k + 1) * cells]
    for slot in range(n):
        outs[slot][...] = dense_ref[pl.ds(slot * tiles, tiles)].astype(outs[slot].dtype)


def total_kernel(n, flux_ref, prior_ref, own_ref, *refs):
    arrived, out_ref = refs[: n - 1], refs[n - 1]
    total = own_ref[...] + prior_ref[...][:, None, :] * flux_ref[...]
    for a in arrived:
        total += a[...].astype(F32)
    out_ref[...] = total


def body(flux_state, prior_precision, footprint, tile_ids, observed, obs_weight):
    n = lax.axis_size("snd")
    windows = lax.axis_size("win")
    flux = flux_state[0]
    tiles, points, cells = flux.shape
    blocks, depth, soundings, _ = footprint.shape
    assert tiles & (tiles - 1) == 0 and tiles % PIECES == 0
    held = (tiles, points, cells)

    rounded = pl.pallas_call(
        round_kernel,
        out_shape=struct(held, BF16),
        in_specs=[HBM],
        out_specs=VMEM,
        scratch_shapes=[pltpu.VMEM(held, F32), pltpu.SemaphoreType.DMA((PIECES,))],
        compiler_params=PARAMS,
        name="round",
    )(in_hbm(flux))
    gather, spread = plans(n, lax.axis_size("pt"))
    shards = [rounded] + [sent(rounded, gather, s) for s in range(n - 1)]
    take, put, foot, turned = pl.pallas_call(
        functools.partial(stage_kernel, gather, spread, tiles),
        out_shape=[struct(tile_ids.shape, I32)] * 2 + [struct(footprint.shape, BF16)] * 2,
        in_specs=[VMEM, HBM],
        out_specs=[VMEM] * 4,
        scratch_shapes=[pltpu.SemaphoreType.DMA((blocks,))],
        compiler_params=PARAMS,
        cost_estimate=pl.CostEstimate(flops=0, transcendentals=0, bytes_accessed=footprint.size * 4),
        name="stage",
    )(tile_ids, in_hbm(footprint))
    mine = pl.pallas_call(
        functools.partial(modeled_kernel, n),
        out_shape=struct((blocks, points, soundings), F32),
        in_specs=[VMEM] * (n + 2),
        out_specs=VMEM,
        scratch_shapes=[pltpu.VMEM((n * tiles, points, cells), BF16)],
        compiler_params=PARAMS,
        name="modeled",
    )(take, turned, *shards)
    if windows == 2:
        other = lax.ppermute(mine, "win", [(0, 1), (1, 0)])
    else:
        other = lax.psum(mine, "win") - mine
    terms = pl.pallas_call(
        functools.partial(terms_kernel, n),
        out_shape=[struct(held, F32)] + [struct(held, BF16)] * (n - 1),
        in_specs=[VMEM] * 6,
        out_specs=[VMEM] * n,
        scratch_shapes=[pltpu.VMEM((n * tiles, points, cells), F32)],
        compiler_params=PARAMS,
        name="terms",
    )(put, mine, other, observed, obs_weight, foot)
    arrived = [sent(terms[s + 1], spread, s) for s in range(n - 1)]
    gradient = pl.pallas_call(
        functools.partial(total_kernel, n),
        out_shape=struct(held, F32),
        in_specs=[VMEM] * (n + 2),
        out_specs=VMEM,
        compiler_params=PARAMS,
        name="total",
    )(flux, prior_precision[0], terms[0], *arrived)
    return gradient[None]


def solution(mesh):
    placed = (
        P(("groups", "win"), "snd", "pt", None),
        P(("groups", "win"), "snd", None),
        P(("groups", "snd"), "win", None, None),
        P(("groups", "snd"), "win"),
        P(("groups", "snd"), None),
        P(("groups", "snd"), None),
    )
    return jax.shard_map(
        body,
        mesh=mesh,
        in_specs=placed,
        out_specs=P(("groups", "win"), "snd", "pt", None),
        check_vma=False,
    )
```

```python
import functools

import jax
import jax.numpy as jnp
from jax import lax
from jax.experimental import pallas as pl
from jax.experimental.pallas import tpu as pltpu
from jax.sharding import PartitionSpec as P

BF16 = jnp.bfloat16
F32 = jnp.float32
I32 = jnp.int32
HBM = pl.BlockSpec(memory_space=pltpu.HBM)
VMEM = pl.BlockSpec(memory_space=pltpu.VMEM)
PARAMS = pltpu.CompilerParams(vmem_limit_bytes=24 << 20)


NEXT, ACROSS, LAST = (1, 2, 3, 0), (2, 3, 0, 1), (3, 0, 1, 2)
CYCLE, MIRROR, BACK = (2, 0, 3, 1), (3, 2, 1, 0), (1, 3, 0, 2)


def plans(n, cores):
    if n == 4 and cores == 2:
        shifts = (NEXT, ACROSS, LAST)
        return ((CYCLE, MIRROR, BACK),) * cores, (shifts, (MIRROR, BACK, CYCLE))
    shifts = tuple(tuple((i + s) % n for i in range(n)) for s in range(1, n))
    return (shifts,) * cores, (shifts,) * cores


def sent(x, plan, step):
    cores = len(plan)
    pairs = [(i * cores + c, to * cores + c) for c, steps in enumerate(plan) for i, to in enumerate(steps[step])]
    return lax.ppermute(x, ("snd", "pt"), pairs)


def slots(plan, owner, arriving):
    n = len(plan[0]) + 1
    me, core = lax.axis_index("snd"), lax.axis_index("pt")
    if all(to == tuple((i + s + 1) % n for i in range(n)) for steps in plan for s, to in enumerate(steps)):
        slot = me - owner if arriving else owner - me
        return jnp.where(slot < 0, slot + n, slot)
    slot = jnp.zeros_like(owner)
    for other in range(n):
        step = jnp.int32(0)
        for c, steps in enumerate(plan):
            for s, to in enumerate(steps):
                source = to.index(other)
                here = to[other] if arriving else source
                step = jnp.where((core == c) & (me == here), s + 1, step)
        slot = jnp.where(owner == other, step, slot)
    return slot


def struct(shape, dtype):
    return jax.ShapeDtypeStruct(shape, dtype)


def in_hbm(x):
    return pltpu.with_memory_space_constraint(x, pltpu.HBM)


def stage(gather, spread, tiles, ids_ref, foot_ref, take_ref, put_ref, foot_out, turned_ref, sems):
    blocks = ids_ref.shape[0]
    first = pltpu.make_async_copy(ids_ref, take_ref, sems.at[blocks])
    first.start()
    copies = [pltpu.make_async_copy(foot_ref.at[b], foot_out.at[b], sems.at[b]) for b in range(blocks)]
    for copy in copies:
        copy.start()
    first.wait()
    ids = take_ref[...]
    shift = tiles.bit_length() - 1
    owner = lax.shift_right_logical(ids, shift)
    local = ids - lax.shift_left(owner, shift)
    take_ref[...] = slots(gather, owner, True) * tiles + local
    put_ref[...] = slots(spread, owner, False) * tiles + local
    for b in range(blocks):
        copies[b].wait()
        turned_ref[b] = jnp.swapaxes(foot_out[b], 1, 2)


def first_kernel(gather, spread, tiles, flux_ref, ids_ref, foot_ref, rounded_ref, *refs):
    staged, (buf_ref, flux_sem, sems) = refs[:4], refs[4:]
    copy = pltpu.make_async_copy(flux_ref, buf_ref, flux_sem)
    copy.start()

    @pl.when(lax.axis_index("pt") == 0)
    def _():
        stage(gather, spread, tiles, ids_ref, foot_ref, *staged, sems)

    copy.wait()
    rounded_ref[...] = buf_ref[...].astype(BF16)


def second_kernel(gather, spread, tiles, ids_ref, foot_ref, *refs):
    early, late, (sems,) = refs[:4], refs[4:8], refs[8:]

    @pl.when(lax.axis_index("pt") != 0)
    def _():
        stage(gather, spread, tiles, ids_ref, foot_ref, *late, sems)

    @pl.when(lax.axis_index("pt") == 0)
    def _():
        copies = [pltpu.make_async_copy(a, b, sems.at[i]) for i, (a, b) in enumerate(zip(early, late))]
        for copy in copies:
            copy.start()
        for copy in copies:
            copy.wait()


def modeled_kernel(n, take_ref, turned_ref, *refs):
    shards = refs[:n]
    out_ref, all_ref = refs[n:]
    tiles = shards[0].shape[0]
    blocks, depth = take_ref.shape
    for slot in range(n):
        all_ref[pl.ds(slot * tiles, tiles)] = shards[slot][...]
    take = take_ref[...]
    for b in range(blocks):
        lhs = jnp.concatenate([all_ref[take[b, k]] for k in range(depth)], axis=1)
        rhs = jnp.concatenate([turned_ref[b, k] for k in range(depth)], axis=0)
        out_ref[b] = jnp.dot(lhs, rhs, preferred_element_type=F32)


def terms_kernel(n, put_ref, mine_ref, other_ref, obs_ref, weight_ref, foot_ref, *refs):
    outs, dense_ref = refs[:n], refs[n]
    tiles = outs[0].shape[0]
    blocks, depth, _, cells = foot_ref.shape
    dense_ref[...] = jnp.zeros_like(dense_ref)
    put = put_ref[...]
    for b in range(blocks):
        modeled = mine_ref[b] + other_ref[b]
        resid = (weight_ref[pl.ds(b, 1), :] * (modeled - obs_ref[pl.ds(b, 1), :])).astype(BF16)
        rhs = jnp.concatenate([foot_ref[b, k] for k in range(depth)], axis=1)
        terms = jnp.dot(resid, rhs, preferred_element_type=F32)
        for k in range(depth):
            dense_ref[put[b, k]] = terms[:, k * cells : (k + 1) * cells]
    for slot in range(n):
        outs[slot][...] = dense_ref[pl.ds(slot * tiles, tiles)].astype(outs[slot].dtype)


def total_kernel(n, flux_ref, prior_ref, own_ref, *refs):
    arrived, out_ref = refs[: n - 1], refs[n - 1]
    total = own_ref[...] + prior_ref[...][:, None, :] * flux_ref[...]
    for a in arrived:
        total += a[...].astype(F32)
    out_ref[...] = total


def body(flux_state, prior_precision, footprint, tile_ids, observed, obs_weight):
    n = lax.axis_size("snd")
    windows = lax.axis_size("win")
    flux = flux_state[0]
    tiles, points, cells = flux.shape
    blocks, depth, soundings, _ = footprint.shape
    assert tiles & (tiles - 1) == 0
    held = (tiles, points, cells)

    gather, spread = plans(n, lax.axis_size("pt"))
    staged = [struct(tile_ids.shape, I32)] * 2 + [struct(footprint.shape, BF16)] * 2
    raw = in_hbm(tile_ids), in_hbm(footprint)
    rounded, *early = pl.pallas_call(
        functools.partial(first_kernel, gather, spread, tiles),
        out_shape=[struct(held, BF16)] + staged,
        in_specs=[HBM] * 3,
        out_specs=[VMEM] * 5,
        scratch_shapes=[
            pltpu.VMEM(held, F32),
            pltpu.SemaphoreType.DMA,
            pltpu.SemaphoreType.DMA((blocks + 1,)),
        ],
        compiler_params=PARAMS,
        name="first",
    )(in_hbm(flux), *raw)
    shards = [rounded] + [sent(rounded, gather, s) for s in range(n - 1)]
    take, put, foot, turned = pl.pallas_call(
        functools.partial(second_kernel, gather, spread, tiles),
        out_shape=staged,
        in_specs=[HBM] * 2 + [VMEM] * 4,
        out_specs=[VMEM] * 4,
        scratch_shapes=[pltpu.SemaphoreType.DMA((blocks + 1,))],
        compiler_params=PARAMS,
        cost_estimate=pl.CostEstimate(flops=0, transcendentals=0, bytes_accessed=footprint.size * 4),
        name="second",
    )(*raw, *early)
    mine = pl.pallas_call(
        functools.partial(modeled_kernel, n),
        out_shape=struct((blocks, points, soundings), F32),
        in_specs=[VMEM] * (n + 2),
        out_specs=VMEM,
        scratch_shapes=[pltpu.VMEM((n * tiles, points, cells), BF16)],
        compiler_params=PARAMS,
        name="modeled",
    )(take, turned, *shards)
    if windows == 2:
        other = lax.ppermute(mine, "win", [(0, 1), (1, 0)])
    else:
        other = lax.psum(mine, "win") - mine
    terms = pl.pallas_call(
        functools.partial(terms_kernel, n),
        out_shape=[struct(held, F32)] + [struct(held, BF16)] * (n - 1),
        in_specs=[VMEM] * 6,
        out_specs=[VMEM] * n,
        scratch_shapes=[pltpu.VMEM((n * tiles, points, cells), F32)],
        compiler_params=PARAMS,
        name="terms",
    )(put, mine, other, observed, obs_weight, foot)
    arrived = [sent(terms[s + 1], spread, s) for s in range(n - 1)]
    gradient = pl.pallas_call(
        functools.partial(total_kernel, n),
        out_shape=struct(held, F32),
        in_specs=[VMEM] * (n + 2),
        out_specs=VMEM,
        compiler_params=PARAMS,
        name="total",
    )(flux, prior_precision[0], terms[0], *arrived)
    return gradient[None]


def solution(mesh):
    placed = (
        P(("groups", "win"), "snd", "pt", None),
        P(("groups", "win"), "snd", None),
        P(("groups", "snd"), "win", None, None),
        P(("groups", "snd"), "win"),
        P(("groups", "snd"), None),
        P(("groups", "snd"), None),
    )
    return jax.shard_map(
        body,
        mesh=mesh,
        in_specs=placed,
        out_specs=P(("groups", "win"), "snd", "pt", None),
        check_vma=False,
    )
```

```python
import functools

import jax
import jax.numpy as jnp
from jax import lax
from jax.experimental import pallas as pl
from jax.experimental.pallas import tpu as pltpu
from jax.sharding import PartitionSpec as P

BF16 = jnp.bfloat16
F32 = jnp.float32
I32 = jnp.int32
HBM = pl.BlockSpec(memory_space=pltpu.HBM)
VMEM = pl.BlockSpec(memory_space=pltpu.VMEM)
PARAMS = pltpu.CompilerParams(vmem_limit_bytes=24 << 20)


NEXT, ACROSS, LAST = (1, 2, 3, 0), (2, 3, 0, 1), (3, 0, 1, 2)
CYCLE, MIRROR, BACK = (2, 0, 3, 1), (3, 2, 1, 0), (1, 3, 0, 2)


def plans(n, cores):
    if n == 4 and cores == 2:
        shifts = (NEXT, ACROSS, LAST)
        return ((CYCLE, MIRROR, BACK),) * cores, (shifts, (MIRROR, BACK, CYCLE))
    shifts = tuple(tuple((i + s) % n for i in range(n)) for s in range(1, n))
    return (shifts,) * cores, (shifts,) * cores


def sent(x, plan, step):
    cores = len(plan)
    pairs = [(i * cores + c, to * cores + c) for c, steps in enumerate(plan) for i, to in enumerate(steps[step])]
    return lax.ppermute(x, ("snd", "pt"), pairs)


def slots(plan, owner, arriving):
    n = len(plan[0]) + 1
    me, core = lax.axis_index("snd"), lax.axis_index("pt")
    if all(to == tuple((i + s + 1) % n for i in range(n)) for steps in plan for s, to in enumerate(steps)):
        slot = me - owner if arriving else owner - me
        return jnp.where(slot < 0, slot + n, slot)
    slot = jnp.zeros_like(owner)
    for other in range(n):
        step = jnp.int32(0)
        for c, steps in enumerate(plan):
            for s, to in enumerate(steps):
                source = to.index(other)
                here = to[other] if arriving else source
                step = jnp.where((core == c) & (me == here), s + 1, step)
        slot = jnp.where(owner == other, step, slot)
    return slot


def struct(shape, dtype):
    return jax.ShapeDtypeStruct(shape, dtype)


def in_hbm(x):
    return pltpu.with_memory_space_constraint(x, pltpu.HBM)


def stage(gather, spread, tiles, ids_ref, foot_ref, take_ref, put_ref, foot_out, turned_ref, sems):
    blocks = ids_ref.shape[0]
    first = pltpu.make_async_copy(ids_ref, take_ref, sems.at[blocks])
    first.start()
    copies = [pltpu.make_async_copy(foot_ref.at[b], foot_out.at[b], sems.at[b]) for b in range(blocks)]
    for copy in copies:
        copy.start()
    first.wait()
    ids = take_ref[...]
    shift = tiles.bit_length() - 1
    owner = lax.shift_right_logical(ids, shift)
    local = ids - lax.shift_left(owner, shift)
    take_ref[...] = slots(gather, owner, True) * tiles + local
    put_ref[...] = slots(spread, owner, False) * tiles + local
    for b in range(blocks):
        copies[b].wait()
        turned_ref[b] = jnp.swapaxes(foot_out[b], 1, 2)


def first_kernel(gather, spread, tiles, flux_ref, ids_ref, foot_ref, rounded_ref, *refs):
    staged, (buf_ref, flux_sem, sems) = refs[:4], refs[4:]
    copy = pltpu.make_async_copy(flux_ref, buf_ref, flux_sem)
    copy.start()

    @pl.when(lax.axis_index("pt") == 0)
    def _():
        stage(gather, spread, tiles, ids_ref, foot_ref, *staged, sems)

    copy.wait()
    rounded_ref[...] = buf_ref[...].astype(BF16)


def second_kernel(gather, spread, tiles, ids_ref, foot_ref, *refs):
    early, late, (sems,) = refs[:4], refs[4:8], refs[8:]

    @pl.when(lax.axis_index("pt") != 0)
    def _():
        stage(gather, spread, tiles, ids_ref, foot_ref, *late, sems)

    @pl.when(lax.axis_index("pt") == 0)
    def _():
        copies = [pltpu.make_async_copy(a, b, sems.at[i]) for i, (a, b) in enumerate(zip(early, late))]
        for copy in copies:
            copy.start()
        for copy in copies:
            copy.wait()


def modeled_kernel(n, take_ref, turned_ref, *refs):
    shards = refs[:n]
    out_ref, all_ref = refs[n:]
    tiles = shards[0].shape[0]
    blocks, depth = take_ref.shape
    for slot in range(n):
        all_ref[pl.ds(slot * tiles, tiles)] = shards[slot][...]
    take = take_ref[...]
    for b in range(blocks):
        lhs = jnp.concatenate([all_ref[take[b, k]] for k in range(depth)], axis=1)
        rhs = jnp.concatenate([turned_ref[b, k] for k in range(depth)], axis=0)
        out_ref[b] = jnp.dot(lhs, rhs, preferred_element_type=F32)


def terms_kernel(n, put_ref, mine_ref, other_ref, obs_ref, weight_ref, foot_ref, *refs):
    outs, dense_ref = refs[:n], refs[n]
    tiles = outs[0].shape[0]
    blocks, depth, _, cells = foot_ref.shape
    dense_ref[...] = jnp.zeros_like(dense_ref)
    put = put_ref[...]
    for b in range(blocks):
        modeled = mine_ref[b] + other_ref[b]
        resid = (weight_ref[pl.ds(b, 1), :] * (modeled - obs_ref[pl.ds(b, 1), :])).astype(BF16)
        rhs = jnp.concatenate([foot_ref[b, k] for k in range(depth)], axis=1)
        terms = jnp.dot(resid, rhs, preferred_element_type=F32)
        for k in range(depth):
            dense_ref[put[b, k]] = terms[:, k * cells : (k + 1) * cells]
    for slot in range(n):
        outs[slot][...] = dense_ref[pl.ds(slot * tiles, tiles)].astype(outs[slot].dtype)


def base_kernel(flux_ref, prior_ref, own_ref, out_ref):
    out_ref[...] = own_ref[...] + prior_ref[...][:, None, :] * flux_ref[...]


def total_kernel(n, base_ref, *refs):
    arrived, out_ref = refs[: n - 1], refs[n - 1]
    total = base_ref[...]
    for a in arrived:
        total += a[...].astype(F32)
    out_ref[...] = total


def body(flux_state, prior_precision, footprint, tile_ids, observed, obs_weight):
    n = lax.axis_size("snd")
    windows = lax.axis_size("win")
    flux = flux_state[0]
    tiles, points, cells = flux.shape
    blocks, depth, soundings, _ = footprint.shape
    assert tiles & (tiles - 1) == 0
    held = (tiles, points, cells)

    gather, spread = plans(n, lax.axis_size("pt"))
    staged = [struct(tile_ids.shape, I32)] * 2 + [struct(footprint.shape, BF16)] * 2
    raw = in_hbm(tile_ids), in_hbm(footprint)
    rounded, *early = pl.pallas_call(
        functools.partial(first_kernel, gather, spread, tiles),
        out_shape=[struct(held, BF16)] + staged,
        in_specs=[HBM] * 3,
        out_specs=[VMEM] * 5,
        scratch_shapes=[
            pltpu.VMEM(held, F32),
            pltpu.SemaphoreType.DMA,
            pltpu.SemaphoreType.DMA((blocks + 1,)),
        ],
        compiler_params=PARAMS,
        name="first",
    )(in_hbm(flux), *raw)
    shards = [rounded] + [sent(rounded, gather, s) for s in range(n - 1)]
    take, put, foot, turned = pl.pallas_call(
        functools.partial(second_kernel, gather, spread, tiles),
        out_shape=staged,
        in_specs=[HBM] * 2 + [VMEM] * 4,
        out_specs=[VMEM] * 4,
        scratch_shapes=[pltpu.SemaphoreType.DMA((blocks + 1,))],
        compiler_params=PARAMS,
        cost_estimate=pl.CostEstimate(flops=0, transcendentals=0, bytes_accessed=footprint.size * 4),
        name="second",
    )(*raw, *early)
    mine = pl.pallas_call(
        functools.partial(modeled_kernel, n),
        out_shape=struct((blocks, points, soundings), F32),
        in_specs=[VMEM] * (n + 2),
        out_specs=VMEM,
        scratch_shapes=[pltpu.VMEM((n * tiles, points, cells), BF16)],
        compiler_params=PARAMS,
        name="modeled",
    )(take, turned, *shards)
    if windows == 2:
        other = lax.ppermute(mine, "win", [(0, 1), (1, 0)])
    else:
        other = lax.psum(mine, "win") - mine
    terms = pl.pallas_call(
        functools.partial(terms_kernel, n),
        out_shape=[struct(held, F32)] + [struct(held, BF16)] * (n - 1),
        in_specs=[VMEM] * 6,
        out_specs=[VMEM] * n,
        scratch_shapes=[pltpu.VMEM((n * tiles, points, cells), F32)],
        compiler_params=PARAMS,
        name="terms",
    )(put, mine, other, observed, obs_weight, foot)
    arrived = [sent(terms[s + 1], spread, s) for s in range(n - 1)]
    base = pl.pallas_call(
        base_kernel,
        out_shape=struct(held, F32),
        in_specs=[VMEM] * 3,
        out_specs=VMEM,
        compiler_params=PARAMS,
        cost_estimate=pl.CostEstimate(flops=0, transcendentals=0, bytes_accessed=footprint.size),
        name="base",
    )(flux, prior_precision[0], terms[0])
    gradient = pl.pallas_call(
        functools.partial(total_kernel, n),
        out_shape=struct(held, F32),
        in_specs=[VMEM] * n,
        out_specs=VMEM,
        compiler_params=PARAMS,
        name="total",
    )(base, *arrived)
    return gradient[None]


def solution(mesh):
    placed = (
        P(("groups", "win"), "snd", "pt", None),
        P(("groups", "win"), "snd", None),
        P(("groups", "snd"), "win", None, None),
        P(("groups", "snd"), "win"),
        P(("groups", "snd"), None),
        P(("groups", "snd"), None),
    )
    return jax.shard_map(
        body,
        mesh=mesh,
        in_specs=placed,
        out_specs=P(("groups", "win"), "snd", "pt", None),
        check_vma=False,
    )
```

```python
import functools

import jax
import jax.numpy as jnp
from jax import lax
from jax.experimental import pallas as pl
from jax.experimental.pallas import tpu as pltpu
from jax.sharding import PartitionSpec as P

BF16 = jnp.bfloat16
F32 = jnp.float32
I32 = jnp.int32
HBM = pl.BlockSpec(memory_space=pltpu.HBM)
VMEM = pl.BlockSpec(memory_space=pltpu.VMEM)
PARAMS = pltpu.CompilerParams(vmem_limit_bytes=24 << 20)


NEXT, ACROSS, LAST = (1, 2, 3, 0), (2, 3, 0, 1), (3, 0, 1, 2)
CYCLE, MIRROR, BACK = (2, 0, 3, 1), (3, 2, 1, 0), (1, 3, 0, 2)


def plans(n, cores):
    if n == 4 and cores == 2:
        shifts = (NEXT, ACROSS, LAST)
        return ((CYCLE, MIRROR, BACK),) * cores, (shifts, (MIRROR, BACK, CYCLE))
    shifts = tuple(tuple((i + s) % n for i in range(n)) for s in range(1, n))
    return (shifts,) * cores, (shifts,) * cores


def sent(x, plan, step):
    cores = len(plan)
    pairs = [(i * cores + c, to * cores + c) for c, steps in enumerate(plan) for i, to in enumerate(steps[step])]
    return lax.ppermute(x, ("snd", "pt"), pairs)


def slots(plan, owner, arriving):
    n = len(plan[0]) + 1
    me, core = lax.axis_index("snd"), lax.axis_index("pt")
    if all(to == tuple((i + s + 1) % n for i in range(n)) for steps in plan for s, to in enumerate(steps)):
        slot = me - owner if arriving else owner - me
        return jnp.where(slot < 0, slot + n, slot)
    slot = jnp.zeros_like(owner)
    for other in range(n):
        step = jnp.int32(0)
        for c, steps in enumerate(plan):
            for s, to in enumerate(steps):
                source = to.index(other)
                here = to[other] if arriving else source
                step = jnp.where((core == c) & (me == here), s + 1, step)
        slot = jnp.where(owner == other, step, slot)
    return slot


def struct(shape, dtype):
    return jax.ShapeDtypeStruct(shape, dtype)


def in_hbm(x):
    return pltpu.with_memory_space_constraint(x, pltpu.HBM)


def stage(gather, spread, tiles, ids_ref, foot_ref, take_ref, put_ref, foot_out, turned_ref, sems):
    blocks = ids_ref.shape[0]
    first = pltpu.make_async_copy(ids_ref, take_ref, sems.at[blocks])
    first.start()
    copies = [pltpu.make_async_copy(foot_ref.at[b], foot_out.at[b], sems.at[b]) for b in range(blocks)]
    for copy in copies:
        copy.start()
    first.wait()
    ids = take_ref[...]
    shift = tiles.bit_length() - 1
    owner = lax.shift_right_logical(ids, shift)
    local = ids - lax.shift_left(owner, shift)
    take_ref[...] = slots(gather, owner, True) * tiles + local
    put_ref[...] = slots(spread, owner, False) * tiles + local
    for b in range(blocks):
        copies[b].wait()
        turned_ref[b] = jnp.swapaxes(foot_out[b], 1, 2)


def first_kernel(gather, spread, tiles, flux_ref, ids_ref, foot_ref, rounded_ref, *refs):
    staged, (buf_ref, flux_sem, sems) = refs[:4], refs[4:]
    copy = pltpu.make_async_copy(flux_ref, buf_ref, flux_sem)
    copy.start()

    @pl.when(lax.axis_index("pt") == 0)
    def _():
        stage(gather, spread, tiles, ids_ref, foot_ref, *staged, sems)

    copy.wait()
    rounded_ref[...] = buf_ref[...].astype(BF16)


def second_kernel(gather, spread, tiles, ids_ref, foot_ref, *refs):
    early, late, (sems,) = refs[:4], refs[4:8], refs[8:]

    @pl.when(lax.axis_index("pt") != 0)
    def _():
        stage(gather, spread, tiles, ids_ref, foot_ref, *late, sems)

    @pl.when(lax.axis_index("pt") == 0)
    def _():
        copies = [pltpu.make_async_copy(a, b, sems.at[i]) for i, (a, b) in enumerate(zip(early, late))]
        for copy in copies:
            copy.start()
        for copy in copies:
            copy.wait()


def modeled_kernel(n, take_ref, turned_ref, *refs):
    shards = refs[:n]
    out_ref, all_ref = refs[n:]
    tiles = shards[0].shape[0]
    blocks, depth = take_ref.shape
    for slot in range(n):
        all_ref[pl.ds(slot * tiles, tiles)] = shards[slot][...]
    take = take_ref[...]
    for b in range(blocks):
        lhs = jnp.concatenate([all_ref[take[b, k]] for k in range(depth)], axis=1)
        rhs = jnp.concatenate([turned_ref[b, k] for k in range(depth)], axis=0)
        out_ref[b] = jnp.dot(lhs, rhs, preferred_element_type=F32)


def terms_kernel(n, put_ref, mine_ref, other_ref, obs_ref, weight_ref, foot_ref, *refs):
    outs, dense_ref = refs[:n], refs[n]
    tiles = outs[0].shape[0]
    blocks, depth, _, cells = foot_ref.shape
    dense_ref[...] = jnp.zeros_like(dense_ref)
    put = put_ref[...]
    for b in range(blocks):
        modeled = mine_ref[b] + other_ref[b]
        resid = (weight_ref[pl.ds(b, 1), :] * (modeled - obs_ref[pl.ds(b, 1), :])).astype(BF16)
        rhs = jnp.concatenate([foot_ref[b, k] for k in range(depth)], axis=1)
        terms = jnp.dot(resid, rhs, preferred_element_type=F32)
        for k in range(depth):
            dense_ref[put[b, k]] = terms[:, k * cells : (k + 1) * cells]
    for slot in range(n):
        outs[slot][...] = dense_ref[pl.ds(slot * tiles, tiles)].astype(outs[slot].dtype)


def base_kernel(flux_ref, prior_ref, own_ref, out_ref):
    out_ref[...] = own_ref[...] + prior_ref[...][:, None, :] * flux_ref[...]


def total_kernel(n, base_ref, *refs):
    arrived, (out_ref, sum_ref, sems) = refs[: n - 1], refs[n - 1 :]
    size = sum_ref.shape[0] // 2
    copies = []
    for i in range(2):
        at = pl.ds(i * size, size)
        total = base_ref[at]
        for a in arrived:
            total += a[at].astype(F32)
        sum_ref[at] = total
        copies.append(pltpu.make_async_copy(sum_ref.at[at], out_ref.at[at], sems.at[i]))
        copies[i].start()
    for copy in copies:
        copy.wait()


def body(flux_state, prior_precision, footprint, tile_ids, observed, obs_weight):
    n = lax.axis_size("snd")
    windows = lax.axis_size("win")
    flux = flux_state[0]
    tiles, points, cells = flux.shape
    blocks, depth, soundings, _ = footprint.shape
    assert tiles & (tiles - 1) == 0
    held = (tiles, points, cells)

    gather, spread = plans(n, lax.axis_size("pt"))
    staged = [struct(tile_ids.shape, I32)] * 2 + [struct(footprint.shape, BF16)] * 2
    raw = in_hbm(tile_ids), in_hbm(footprint)
    rounded, *early = pl.pallas_call(
        functools.partial(first_kernel, gather, spread, tiles),
        out_shape=[struct(held, BF16)] + staged,
        in_specs=[HBM] * 3,
        out_specs=[VMEM] * 5,
        scratch_shapes=[
            pltpu.VMEM(held, F32),
            pltpu.SemaphoreType.DMA,
            pltpu.SemaphoreType.DMA((blocks + 1,)),
        ],
        compiler_params=PARAMS,
        name="first",
    )(in_hbm(flux), *raw)
    shards = [rounded] + [sent(rounded, gather, s) for s in range(n - 1)]
    take, put, foot, turned = pl.pallas_call(
        functools.partial(second_kernel, gather, spread, tiles),
        out_shape=staged,
        in_specs=[HBM] * 2 + [VMEM] * 4,
        out_specs=[VMEM] * 4,
        scratch_shapes=[pltpu.SemaphoreType.DMA((blocks + 1,))],
        compiler_params=PARAMS,
        cost_estimate=pl.CostEstimate(flops=0, transcendentals=0, bytes_accessed=footprint.size * 4),
        name="second",
    )(*raw, *early)
    mine = pl.pallas_call(
        functools.partial(modeled_kernel, n),
        out_shape=struct((blocks, points, soundings), F32),
        in_specs=[VMEM] * (n + 2),
        out_specs=VMEM,
        scratch_shapes=[pltpu.VMEM((n * tiles, points, cells), BF16)],
        compiler_params=PARAMS,
        name="modeled",
    )(take, turned, *shards)
    if windows == 2:
        other = lax.ppermute(mine, "win", [(0, 1), (1, 0)])
    else:
        other = lax.psum(mine, "win") - mine
    terms = pl.pallas_call(
        functools.partial(terms_kernel, n),
        out_shape=[struct(held, F32)] + [struct(held, BF16)] * (n - 1),
        in_specs=[VMEM] * 6,
        out_specs=[VMEM] * n,
        scratch_shapes=[pltpu.VMEM((n * tiles, points, cells), F32)],
        compiler_params=PARAMS,
        name="terms",
    )(put, mine, other, observed, obs_weight, foot)
    arrived = [sent(terms[s + 1], spread, s) for s in range(n - 1)]
    base = pl.pallas_call(
        base_kernel,
        out_shape=struct(held, F32),
        in_specs=[VMEM] * 3,
        out_specs=VMEM,
        compiler_params=PARAMS,
        cost_estimate=pl.CostEstimate(flops=0, transcendentals=0, bytes_accessed=footprint.size),
        name="base",
    )(flux, prior_precision[0], terms[0])
    gradient = pl.pallas_call(
        functools.partial(total_kernel, n),
        out_shape=struct(held, F32),
        in_specs=[VMEM] * n,
        out_specs=HBM,
        scratch_shapes=[pltpu.VMEM(held, F32), pltpu.SemaphoreType.DMA((2,))],
        compiler_params=PARAMS,
        name="total",
    )(base, *arrived)
    return gradient[None]


def solution(mesh):
    placed = (
        P(("groups", "win"), "snd", "pt", None),
        P(("groups", "win"), "snd", None),
        P(("groups", "snd"), "win", None, None),
        P(("groups", "snd"), "win"),
        P(("groups", "snd"), None),
        P(("groups", "snd"), None),
    )
    return jax.shard_map(
        body,
        mesh=mesh,
        in_specs=placed,
        out_specs=P(("groups", "win"), "snd", "pt", None),
        check_vma=False,
    )
```
